32 devices in a mesh: row: 8 (over y, x, core), col: 4 (over z).
Axes of the slice: x: 2, y: 2, z: 4, core: 2. Of those that a mesh axis runs over, the one named last changes fastest.
Arguments:
- features: bfloat16 [4096, 512], P(('row', 'col')), may hold values from -6 to 6
- weight: bfloat16 [512, 512], replicated, may hold values from -0.25 to 0.25
- cotangent: bfloat16 [4096, 512], P(('row', 'col')), may hold values from -6 to 6
- tile_blocks: bfloat16 [64, 128, 128], P(('row', 'col')), may hold values from -0.25 to 0.25
- tile_index: int32 [32, 2], P(('row', 'col')), may hold values from 0 to 3, as said below
- tile_count: int32 [32], P(('row', 'col')), may hold values from 1 to 2, as said below
Outputs:
- out_features: bfloat16 [4096, 512], P(('row', 'col'))
- grad_features: bfloat16 [4096, 512], P(('row', 'col'))
- grad_weight: float32 [512, 512], P('col')
The draws below stay inside these ranges and needn't reach their ends.
Inputs may be any that keep to these rules, and one draw needn't show every extreme that they name: `tile_index`: in each block's row the first tile_count entries are strictly increasing, and all 2 entries are distinct; slots at or past tile_count are ignored. `tile_count`: some block has exactly 2 live slots.
All inputs are finite; a program needn't handle non-finite values.
Results may differ from the reference program's by a relative error of at most 0.007.
Values may be sent and summed in bfloat16 or wider, within the bound.
No kernel may reach another device: no remote copies, remote signals or barrier semaphores. Data moves between devices by JAX's collectives and lax.ppermute only.
A program may use at most 64 MiB of HBM per device.

```python
import math
import jax
import jax.numpy as jnp
from jax import lax

H = 512
TILE = 128
ROW_TILES = 1
COL_TILES = 4
MAX_TILES = 2
NODES = 4096
N_ROW = 8
N_COL = 4


def count_law(key):
    base = jax.random.fold_in(key, 11)
    first_key, second_key = jax.random.split(base)
    levels = jax.random.randint(first_key, (N_ROW * N_COL,), 1, 9)
    counts = jnp.maximum(1, MAX_TILES * levels * levels // 64)
    heavy = jax.random.randint(second_key, (), 0, N_ROW * N_COL)
    counts = jnp.where(jnp.arange(N_ROW * N_COL) == heavy, MAX_TILES, counts)
    return counts.astype(jnp.int32)


def draw_tile_count(key, part):
    return count_law(key)


def draw_tile_index(key, part):
    counts = count_law(key)
    total = ROW_TILES * COL_TILES
    block_keys = jax.random.split(jax.random.fold_in(key, 23), N_ROW * N_COL)
    chosen = jax.vmap(lambda one_key: jax.random.permutation(one_key, total)[:MAX_TILES])(block_keys)
    live = jnp.arange(MAX_TILES)[None, :] < counts[:, None]
    ordered = jnp.sort(jnp.where(live, chosen, chosen + total), axis=1)
    return jnp.where(ordered >= total, ordered - total, ordered).astype(jnp.int32)


def raised(drawn, rng, source, target, parts, factor):
    def block_of(dim):
        return (jnp.arange(drawn.shape[dim]) // (drawn.shape[dim] // parts)).reshape((-1,) + (1,) * (drawn.ndim - 1 - dim))

    near = jax.random.permutation(rng, parts)[block_of(target)]
    second = (block_of(target) + parts // 2) % parts
    return jnp.where((block_of(source) == near) | (block_of(source) == second), factor * drawn, drawn)


def block_levels(stream_key, extent, pieces, low, largest):
    gain, own = 1.0, jax.random.fold_in(stream_key, 6)
    for position, parts in pieces:
        draws = jnp.exp(jax.random.uniform(jax.random.fold_in(own, position), (parts,), jnp.float32, low / len(pieces), largest / len(pieces)))
        gain = gain * jnp.repeat(draws, extent[position] // parts).reshape([-1 if axis == position else 1 for axis in range(len(extent))])
    return gain


def bell_draw(own_key, shape, spread, bound, pieces=(), held_as=jnp.bfloat16):
    result = spread * jax.random.normal(own_key, shape, jnp.float32)
    if pieces:
        result = result * block_levels(own_key, shape, pieces, -0.22, 0.18)
    return jnp.clip(result, -bound, bound).astype(held_as)


def noise_with(key, extent, deviation, reach, shards, heavy, held_as=jnp.bfloat16):
    entries = deviation * jax.random.normal(key, extent, jnp.float32)
    if shards:
        entries = entries * block_levels(key, extent, shards, -0.22, 0.18)
    return jnp.clip(raised(entries, jax.random.fold_in(key, 3), *heavy), -reach, reach).astype(held_as)


def setup_inputs(seed: int = 0) -> dict:
    arg_keys = jax.random.split(jax.random.key(seed), 7)
    return {
        "features": noise_with(arg_keys[0], (NODES, H), 1.0, 6.0, ((0, 32),), (0, 1, 32, 2.75)),
        "weight": bell_draw(arg_keys[1], (H, H), H ** -0.5, 0.25),
        "cotangent": bell_draw(arg_keys[2], (NODES, H), 1.0, 6.0, ((0, 32),)),
        "tile_blocks": bell_draw(arg_keys[3], (N_ROW * N_COL * MAX_TILES, TILE, TILE), (4 * TILE) ** -0.5, 0.25, ((0, 32),)),
        "tile_index": draw_tile_index(jax.random.fold_in(arg_keys[6], 71), 0),
        "tile_count": draw_tile_count(jax.random.fold_in(arg_keys[6], 71), 0),
    }


def cluster_forward(panels, blocks, index, live_count, column):
    own = lax.dynamic_slice_in_dim(panels, column * ROW_TILES, ROW_TILES, 0).astype(jnp.float32)

    def step(slot, acc):
        place = index[slot]
        block = blocks[slot].astype(jnp.float32)
        source = panels[place // ROW_TILES].astype(jnp.float32)
        return acc.at[place % ROW_TILES].add(jnp.dot(block, source, preferred_element_type=jnp.float32))
    return lax.fori_loop(0, live_count, step, own)

def reference(features, weight, cotangent, tile_blocks, tile_index, tile_count):
    panels = features.reshape(N_ROW, COL_TILES, TILE, H)
    blocks = tile_blocks.reshape(N_ROW, N_COL, MAX_TILES, TILE, TILE)
    index = tile_index.reshape(N_ROW, N_COL, MAX_TILES)
    counts = tile_count.reshape(N_ROW, N_COL)
    columns = jnp.arange(N_COL, dtype=jnp.int32)

    def forward_group(group):
        group_panels, group_blocks, group_index, group_counts = group

        def one_block(item):
            return cluster_forward(group_panels, item[0], item[1], item[2], item[3])
        return lax.map(one_block, (group_blocks, group_index, group_counts, columns))
    summed = lax.map(forward_group, (panels, blocks, index, counts))
    aggregated = summed.reshape(NODES, H).astype(jnp.bfloat16)
    pre_act = jnp.dot(aggregated, weight, preferred_element_type=jnp.float32)
    sigmoid_pre = jax.nn.sigmoid(pre_act)
    out_features = (pre_act * sigmoid_pre).astype(jnp.bfloat16)
    grad_pre = (cotangent.astype(jnp.float32) * sigmoid_pre * (1.0 + pre_act * (1.0 - sigmoid_pre))).astype(jnp.bfloat16)
    grad_weight = jnp.dot(aggregated.T, grad_pre, preferred_element_type=jnp.float32) * (1.0 / math.sqrt(NODES))
    grad_mid = jnp.dot(grad_pre, weight.T, preferred_element_type=jnp.float32).astype(jnp.bfloat16)
    mids = grad_mid.reshape(N_ROW, N_COL, ROW_TILES, TILE, H)

    def backward_group(group):
        group_mids, group_blocks, group_index, group_counts = group

        def add_block(total, item):
            own_mid, blocks_one, index_one, count_one = item

            def step(slot, acc):
                place = index_one[slot]
                block = blocks_one[slot].astype(jnp.float32)
                source = own_mid[place % ROW_TILES].astype(jnp.float32)
                return acc.at[place // ROW_TILES].add(jnp.dot(block.T, source, preferred_element_type=jnp.float32))
            partial_value = lax.fori_loop(0, count_one, step, jnp.zeros((COL_TILES, TILE, H), jnp.float32))
            rounded = lax.optimization_barrier(partial_value.astype(jnp.bfloat16)).astype(jnp.float32)
            return (total + rounded, None)
        total, unused = lax.scan(add_block, jnp.zeros((COL_TILES, TILE, H), jnp.float32), (group_mids, group_blocks, group_index, group_counts))
        return total
    sums = lax.map(backward_group, (mids, blocks, index, counts))
    grad_features = (grad_mid.astype(jnp.float32) + sums.reshape(NODES, H)).astype(jnp.bfloat16)
    return (out_features, grad_features, grad_weight)
```

```python
import functools
import math

import jax
import jax.numpy as jnp
from jax import lax
from jax.experimental import pallas as pl
from jax.experimental.pallas import tpu as pltpu
from jax.sharding import PartitionSpec as P

F32 = jnp.float32
BF16 = jnp.bfloat16


def tile_range(tile_col, live_mask, first, extent):
    lower = jnp.sum(jnp.where(live_mask & (tile_col < first), 1, 0)).astype(jnp.int32)
    upper = jnp.sum(jnp.where(live_mask & (tile_col < first + extent), 1, 0)).astype(jnp.int32)
    return (lower, upper)


def any_mesh(features, weight, cotangent, tile_blocks, tile_index, tile_count):
    rows, width = features.shape
    tile = tile_blocks.shape[1]
    row_tiles = rows // tile
    slots = tile_blocks.shape[0]
    index = tile_index[0]
    live_mask = jnp.arange(slots, dtype=jnp.int32) < tile_count[0]
    tile_col = index // row_tiles
    tile_row = index % row_tiles
    panels = features.reshape(row_tiles, tile, width)
    piece = lax.all_gather(panels, "col", axis=0, tiled=True)
    lower, upper = tile_range(tile_col, live_mask, jnp.int32(0), piece.shape[0])

    def add_step(slot, acc):
        block = lax.dynamic_index_in_dim(tile_blocks, slot, 0, keepdims=False)
        source = lax.dynamic_index_in_dim(piece, tile_col[slot], 0, keepdims=False)
        product = jnp.dot(block, source, preferred_element_type=F32)
        current = lax.dynamic_index_in_dim(acc, tile_row[slot], 0, keepdims=False)
        return lax.dynamic_update_index_in_dim(acc, current + product, tile_row[slot], 0)

    summed = lax.fori_loop(lower, upper, add_step, panels.astype(F32))
    aggregated = summed.reshape(rows, width).astype(BF16)
    pre_act = jnp.dot(aggregated, weight, preferred_element_type=F32)
    sigmoid_pre = jax.nn.sigmoid(pre_act)
    out_features = (pre_act * sigmoid_pre).astype(BF16)
    grad_pre = (
        cotangent.astype(F32) * sigmoid_pre * (1.0 + pre_act * (1.0 - sigmoid_pre))
    ).astype(BF16)
    node_total = rows * lax.axis_size("row") * lax.axis_size("col")
    local_weight = lax.dot_general(
        aggregated, grad_pre, (((0,), (0,)), ((), ())), preferred_element_type=F32
    ) * (1.0 / math.sqrt(node_total))
    grad_mid = lax.dot_general(
        grad_pre, weight, (((1,), (1,)), ((), ())), preferred_element_type=F32
    ).astype(BF16)
    mid_tiles = grad_mid.reshape(row_tiles, tile, width)
    extent = lax.axis_size("col") * rows
    first = jnp.int32(0) // tile
    tiles_here = extent // tile
    lower, upper = tile_range(tile_col, live_mask, first, tiles_here)

    def spread_step(slot, acc):
        block = lax.dynamic_index_in_dim(tile_blocks, slot, 0, keepdims=False)
        source = lax.dynamic_index_in_dim(mid_tiles, tile_row[slot], 0, keepdims=False)
        product = lax.dot_general(
            block, source, (((0,), (0,)), ((), ())), preferred_element_type=F32
        )
        target = tile_col[slot]
        current = lax.dynamic_index_in_dim(acc, target, 0, keepdims=False)
        return lax.dynamic_update_index_in_dim(acc, current + product, target, 0)

    terms = lax.fori_loop(
        lower, upper, spread_step, jnp.zeros((tiles_here, tile, width), F32)
    )
    gathered_back = lax.psum_scatter(
        terms.reshape(extent, width).astype(BF16), "col", scatter_dimension=0, tiled=True
    ).astype(F32)
    grad_features = (grad_mid.astype(F32) + gathered_back).astype(BF16)
    share = width // lax.axis_size("col")
    total_weight = lax.psum(local_weight, ("row", "col"))
    grad_weight = lax.dynamic_slice_in_dim(total_weight, lax.axis_index("col") * share, share, 0)
    return (out_features, grad_features, grad_weight)


def swap(value, axis, mask, size):
    return lax.ppermute(value, axis, [(i, i ^ mask) for i in range(size)])


def vmem(count):
    return [pl.BlockSpec(memory_space=pltpu.VMEM)] * count


def forward_kernel(scale, slots, where, f0, f1, f2, f3, tp0, tp1, ct0, ct1, w,
                   out, gp, sel, keep, send, adj, agg, gw):
    tile = f0.shape[0]
    own, half = where[0], where[1]
    for b, tp in enumerate((tp0, tp1)):
        for t in range(4):
            name = (own ^ t).astype(F32)
            total = jnp.zeros((tile, tile), BF16)
            for s in range(slots):
                mark = tp[pl.ds(slots * tile + 16 * s, 16), :][0:1, :].astype(F32)
                block = tp[pl.ds(s * tile, tile), :]
                total = total + jnp.where(mark == name, block.astype(F32), 0.0).astype(BF16)
            adj[pl.ds(b * tile, tile), pl.ds(t * tile, tile)] = total
    near = jnp.concatenate([f0[...], f1[...]], axis=0)
    far = jnp.concatenate([f2[...], f3[...]], axis=0)
    summed = near.astype(F32)
    summed = summed + jnp.dot(adj[:, : 2 * tile], near, preferred_element_type=F32)
    summed = summed + jnp.dot(adj[:, 2 * tile :], far, preferred_element_type=F32)
    agg[...] = summed.astype(BF16)
    pre = jnp.dot(agg[...], w[...], preferred_element_type=F32)
    sig = jax.nn.sigmoid(pre)
    out[...] = (pre[:tile] * sig[:tile]).astype(BF16)
    cot = jnp.concatenate([ct0[...], ct1[...]], axis=0).astype(F32)
    gp[...] = (cot * sig * (1.0 + pre * (1.0 - sig))).astype(BF16)
    sel[:, :tile] = adj[:, :tile]
    sel[:, tile:] = adj[:, 2 * tile : 3 * tile]
    for b in range(2):
        lane = pl.multiple_of((own ^ (2 * b)) * tile, tile)
        gw[pl.ds(b * tile, tile), :] = lax.dot_general(
            agg[:, pl.ds(lane, tile)], gp[...], (((0,), (0,)), ((), ())),
            preferred_element_type=F32,
        ) * scale
        part = tile // 2
        mine = pl.multiple_of(b * tile + half * part, part)
        other = pl.multiple_of(b * tile + (1 - half) * part, part)
        keep[b] = gw[pl.ds(mine, part), :]
        send[b] = gw[pl.ds(other, part), :].astype(BF16)


def backward_kernel(gp, sel, w, back, part):
    tile = gp.shape[0] // 2
    mid = lax.dot_general(
        gp[...], w[...], (((1,), (1,)), ((), ())), preferred_element_type=F32
    ).astype(BF16)
    terms = lax.dot_general(
        sel[...], mid, (((0,), (0,)), ((), ())), preferred_element_type=F32
    )
    back[...] = terms[tile:].astype(BF16)
    part[...] = mid[:tile].astype(F32) + terms[:tile]


def four_by_eight(features, weight, cotangent, tile_blocks, tile_index, tile_count):
    rows, width = features.shape
    slots, tile, _ = tile_blocks.shape
    own = lax.axis_index("col")
    half = lax.axis_index("row") & 1
    f3 = swap(features, "col", 3, 4)
    f2 = swap(features, "col", 2, 4)
    f1 = swap(features, "col", 1, 4)
    ct1 = swap(cotangent, "col", 1, 4)
    live = jnp.arange(slots, dtype=jnp.int32) < tile_count[0]
    marks = jnp.where(live, tile_index[0], -1).astype(BF16)
    marks = jnp.broadcast_to(marks[:, None, None], (slots, 16, tile)).reshape(slots * 16, tile)
    tp0 = jnp.concatenate([tile_blocks.reshape(slots * tile, tile), marks], axis=0)
    tp1 = swap(tp0, "col", 1, 4)
    where = jnp.stack([own, half]).astype(jnp.int32)
    scale = 1.0 / math.sqrt(rows * lax.axis_size("row") * lax.axis_size("col"))
    out, gp, sel, keep, send = pl.pallas_call(
        functools.partial(forward_kernel, scale, slots),
        out_shape=(
            jax.ShapeDtypeStruct((rows, width), BF16),
            jax.ShapeDtypeStruct((2 * rows, width), BF16),
            jax.ShapeDtypeStruct((2 * rows, 2 * tile), BF16),
            jax.ShapeDtypeStruct((2, tile // 2, width), F32),
            jax.ShapeDtypeStruct((2, tile // 2, width), BF16),
        ),
        in_specs=[pl.BlockSpec(memory_space=pltpu.SMEM)] + vmem(9),
        out_specs=tuple(vmem(5)),
        scratch_shapes=[
            pltpu.VMEM((2 * tile, 4 * tile), BF16),
            pltpu.VMEM((2 * tile, width), BF16),
            pltpu.VMEM((2 * tile, width), F32),
        ],
        cost_estimate=pl.CostEstimate(
            flops=2 * 256 * 512 * 512 * 3, bytes_accessed=3 << 20, transcendentals=256 * 512
        ),
    )(where, features, f1, f2, f3, tp0, tp1, cotangent, ct1, weight)
    got = swap(send, "row", 1, 8)
    summed = keep + got.astype(F32)
    got = swap(summed[1].astype(BF16), "col", 2, 4)
    mine = (summed[0] + got.astype(F32)).astype(BF16)
    back, part = pl.pallas_call(
        backward_kernel,
        out_shape=(
            jax.ShapeDtypeStruct((rows, width), BF16),
            jax.ShapeDtypeStruct((rows, width), F32),
        ),
        in_specs=vmem(3),
        out_specs=tuple(vmem(2)),
        cost_estimate=pl.CostEstimate(
            flops=2 * 256 * 512 * 512 * 2, bytes_accessed=2 << 20, transcendentals=0
        ),
    )(gp, sel, weight)
    got_back = swap(back, "col", 2, 4)
    diagonal = swap(mine, "row", 6, 8).astype(F32)
    along = swap(mine, "row", 4, 8).astype(F32)
    across = swap(mine, "row", 2, 8).astype(F32)
    total = (mine.astype(F32) + across) + (along + diagonal)
    rest = swap(total, "row", 1, 8)
    first = jnp.where(half == 0, total, rest)
    second = jnp.where(half == 0, rest, total)
    grad_weight = jnp.concatenate([first, second], axis=0)
    grad_features = (part + got_back.astype(F32)).astype(BF16)
    return (out, grad_features, grad_weight)


def solution(mesh):
    sizes = (mesh.shape["row"], mesh.shape["col"])

    def on_device(*args):
        rows, width = args[0].shape
        tile = args[3].shape[1]
        small = sizes == (8, 4) and rows == tile and width == 4 * tile
        return (four_by_eight if small else any_mesh)(*args)

    return jax.shard_map(
        on_device,
        mesh=mesh,
        in_specs=(
            P(("row", "col"), None),
            P(),
            P(("row", "col"), None),
            P(("row", "col"), None, None),
            P(("row", "col"), None),
            P(("row", "col")),
        ),
        out_specs=(P(("row", "col"), None), P(("row", "col"), None), P("col", None)),
        check_vma=False,
    )
```

```python
import functools
import math

import jax
import jax.numpy as jnp
from jax import lax
from jax.experimental import pallas as pl
from jax.experimental.pallas import tpu as pltpu
from jax.sharding import PartitionSpec as P

F32 = jnp.float32
BF16 = jnp.bfloat16


def tile_range(tile_col, live_mask, first, extent):
    lower = jnp.sum(jnp.where(live_mask & (tile_col < first), 1, 0)).astype(jnp.int32)
    upper = jnp.sum(jnp.where(live_mask & (tile_col < first + extent), 1, 0)).astype(jnp.int32)
    return (lower, upper)


def any_mesh(features, weight, cotangent, tile_blocks, tile_index, tile_count):
    rows, width = features.shape
    tile = tile_blocks.shape[1]
    row_tiles = rows // tile
    slots = tile_blocks.shape[0]
    index = tile_index[0]
    live_mask = jnp.arange(slots, dtype=jnp.int32) < tile_count[0]
    tile_col = index // row_tiles
    tile_row = index % row_tiles
    panels = features.reshape(row_tiles, tile, width)
    piece = lax.all_gather(panels, "col", axis=0, tiled=True)
    lower, upper = tile_range(tile_col, live_mask, jnp.int32(0), piece.shape[0])

    def add_step(slot, acc):
        block = lax.dynamic_index_in_dim(tile_blocks, slot, 0, keepdims=False)
        source = lax.dynamic_index_in_dim(piece, tile_col[slot], 0, keepdims=False)
        product = jnp.dot(block, source, preferred_element_type=F32)
        current = lax.dynamic_index_in_dim(acc, tile_row[slot], 0, keepdims=False)
        return lax.dynamic_update_index_in_dim(acc, current + product, tile_row[slot], 0)

    summed = lax.fori_loop(lower, upper, add_step, panels.astype(F32))
    aggregated = summed.reshape(rows, width).astype(BF16)
    pre_act = jnp.dot(aggregated, weight, preferred_element_type=F32)
    sigmoid_pre = jax.nn.sigmoid(pre_act)
    out_features = (pre_act * sigmoid_pre).astype(BF16)
    grad_pre = (
        cotangent.astype(F32) * sigmoid_pre * (1.0 + pre_act * (1.0 - sigmoid_pre))
    ).astype(BF16)
    node_total = rows * lax.axis_size("row") * lax.axis_size("col")
    local_weight = lax.dot_general(
        aggregated, grad_pre, (((0,), (0,)), ((), ())), preferred_element_type=F32
    ) * (1.0 / math.sqrt(node_total))
    grad_mid = lax.dot_general(
        grad_pre, weight, (((1,), (1,)), ((), ())), preferred_element_type=F32
    ).astype(BF16)
    mid_tiles = grad_mid.reshape(row_tiles, tile, width)
    extent = lax.axis_size("col") * rows
    first = jnp.int32(0) // tile
    tiles_here = extent // tile
    lower, upper = tile_range(tile_col, live_mask, first, tiles_here)

    def spread_step(slot, acc):
        block = lax.dynamic_index_in_dim(tile_blocks, slot, 0, keepdims=False)
        source = lax.dynamic_index_in_dim(mid_tiles, tile_row[slot], 0, keepdims=False)
        product = lax.dot_general(
            block, source, (((0,), (0,)), ((), ())), preferred_element_type=F32
        )
        target = tile_col[slot]
        current = lax.dynamic_index_in_dim(acc, target, 0, keepdims=False)
        return lax.dynamic_update_index_in_dim(acc, current + product, target, 0)

    terms = lax.fori_loop(
        lower, upper, spread_step, jnp.zeros((tiles_here, tile, width), F32)
    )
    gathered_back = lax.psum_scatter(
        terms.reshape(extent, width).astype(BF16), "col", scatter_dimension=0, tiled=True
    ).astype(F32)
    grad_features = (grad_mid.astype(F32) + gathered_back).astype(BF16)
    share = width // lax.axis_size("col")
    total_weight = lax.psum(local_weight, ("row", "col"))
    grad_weight = lax.dynamic_slice_in_dim(total_weight, lax.axis_index("col") * share, share, 0)
    return (out_features, grad_features, grad_weight)


def swap(value, axis, mask, size):
    return lax.ppermute(value, axis, [(i, i ^ mask) for i in range(size)])


def vmem(count):
    return [pl.BlockSpec(memory_space=pltpu.VMEM)] * count


def place(adj, row, tp, own, slots):
    tile = tp.shape[1]
    for t in range(4):
        name = (own ^ t).astype(F32)
        total = jnp.zeros((tile, tile), F32)
        for s in range(slots):
            mark = tp[pl.ds(slots * tile + 16 * s, 16), :][0:1, :].astype(F32)
            block = tp[pl.ds(s * tile, tile), :]
            total = total + jnp.where(mark == name, block.astype(F32), 0.0)
        adj[pl.ds(row, tile), pl.ds(t * tile, tile)] = total.astype(BF16)


def stage_kernel(slots, where, tp, f, ct, w, f_out, ct_out, w_out, adj):
    place(adj, 0, tp, where[0], slots)
    f_out[...] = f[...]
    ct_out[...] = ct[...]
    w_out[...] = w[...]


def activate(adj, near, far, own_rows, ct, w):
    half = near.shape[0]
    summed = own_rows.astype(F32)
    summed = summed + jnp.dot(adj[:, :half], near, preferred_element_type=F32)
    summed = summed + jnp.dot(adj[:, half:], far, preferred_element_type=F32)
    agg = summed.astype(BF16)
    pre = jnp.dot(agg, w, preferred_element_type=F32)
    sig = jax.nn.sigmoid(pre)
    slope = ct.astype(F32) * sig * (1.0 + pre * (1.0 - sig))
    return agg, (pre * sig).astype(BF16), slope.astype(BF16)


def own_kernel(f0, f1, f2, f3, adj, ct, w, out, agg, gp, near, far):
    tile = f1.shape[0]
    near[:tile], near[tile:] = f0[...], f1[...]
    far[:tile], far[tile:] = f2[...], f3[...]
    agg[...], out[...], gp[...] = activate(adj[...], near[...], far[...], f0[...], ct[...], w[...])


def pair_kernel(scale, slots, where, near, far, tp, ct, w, agg0, gp0,
                gp1, adj, keep, send, agg, gp, gw):
    tile = tp.shape[1]
    own, half = where[0], where[1]
    place(adj, 0, tp, own, slots)
    agg[:tile], gp[:tile] = agg0[...], gp0[...]
    agg1, _, slope = activate(adj[...], near[...], far[...], near[tile:], ct[...], w[...])
    agg[tile:], gp[tile:], gp1[...] = agg1, slope, slope
    part = tile // 2
    for b in range(2):
        lane = pl.multiple_of((own ^ (2 * b)) * tile, tile)
        gw[pl.ds(b * tile, tile), :] = lax.dot_general(
            agg[:, pl.ds(lane, tile)], gp[...], (((0,), (0,)), ((), ())),
            preferred_element_type=F32,
        ) * scale
        mine = pl.multiple_of(b * tile + half * part, part)
        other = pl.multiple_of(b * tile + (1 - half) * part, part)
        keep[b] = gw[pl.ds(mine, part), :]
        send[b] = gw[pl.ds(other, part), :].astype(BF16)


def pack_kernel(index, count, blocks, packed):
    slots, tile, _ = blocks.shape
    for s in range(slots):
        packed[pl.ds(s * tile, tile), :] = blocks[s]
        mark = jnp.where(s < count[0], index[0, s], -1).astype(F32)
        packed[pl.ds(slots * tile + 16 * s, 16), :] = jnp.full((16, tile), mark, F32).astype(BF16)


def backward_kernel(gp0, gp1, adj0, adj1, w, back, part):
    tile = gp0.shape[0]
    terms = jnp.zeros((2 * tile, w.shape[0]), F32)
    for b, (gp, adj) in enumerate(((gp0, adj0), (gp1, adj1))):
        mid = lax.dot_general(
            gp[...], w[...], (((1,), (1,)), ((), ())), preferred_element_type=F32
        ).astype(BF16)
        sel = jnp.concatenate([adj[:, :tile], adj[:, 2 * tile : 3 * tile]], axis=1)
        terms = terms + lax.dot_general(
            sel, mid, (((0,), (0,)), ((), ())), preferred_element_type=F32
        )
        if b == 0:
            part[...] = mid.astype(F32)
    back[...] = terms[tile:].astype(BF16)
    part[...] = part[...] + terms[:tile]


def four_by_eight(features, weight, cotangent, tile_blocks, tile_index, tile_count):
    rows, width = features.shape
    slots, tile, _ = tile_blocks.shape
    own = lax.axis_index("col")
    half = lax.axis_index("row") & 1
    where = jnp.stack([own, half]).astype(jnp.int32)
    f3 = swap(features, "col", 3, 4)
    f2 = swap(features, "col", 2, 4)
    f1 = swap(features, "col", 1, 4)
    ct1 = swap(cotangent, "col", 1, 4)
    tp0 = pl.pallas_call(
        pack_kernel,
        out_shape=jax.ShapeDtypeStruct((slots * (tile + 16), tile), BF16),
        in_specs=[pl.BlockSpec(memory_space=pltpu.SMEM)] * 2 + vmem(1),
        out_specs=vmem(1)[0],
        compiler_params=pltpu.CompilerParams(vmem_limit_bytes=2 << 20),
    )(tile_index, tile_count, tile_blocks)
    tp1 = swap(tp0, "col", 1, 4)
    f0, ct0, w, adj0 = pl.pallas_call(
        functools.partial(stage_kernel, slots),
        out_shape=(
            jax.ShapeDtypeStruct((rows, width), BF16),
            jax.ShapeDtypeStruct((rows, width), BF16),
            jax.ShapeDtypeStruct((width, width), BF16),
            jax.ShapeDtypeStruct((tile, 4 * tile), BF16),
        ),
        in_specs=[pl.BlockSpec(memory_space=pltpu.SMEM)] + vmem(4),
        out_specs=tuple(vmem(4)),
        compiler_params=pltpu.CompilerParams(vmem_limit_bytes=8 << 20),
    )(where, tp0, features, cotangent, weight)
    scale = 1.0 / math.sqrt(rows * lax.axis_size("row") * lax.axis_size("col"))
    block = jax.ShapeDtypeStruct((rows, width), BF16)
    double = jax.ShapeDtypeStruct((2 * rows, width), BF16)
    out, agg0, gp0, near, far = pl.pallas_call(
        own_kernel,
        out_shape=(block, block, block, double, double),
        in_specs=vmem(7),
        out_specs=tuple(vmem(5)),
        compiler_params=pltpu.CompilerParams(vmem_limit_bytes=8 << 20),
        cost_estimate=pl.CostEstimate(
            flops=4 * rows * width * width, bytes_accessed=1 << 20, transcendentals=rows * width
        ),
    )(f0, f1, f2, f3, adj0, ct0, w)
    gp1, adj1, keep, send = pl.pallas_call(
        functools.partial(pair_kernel, scale, slots),
        out_shape=(
            block,
            jax.ShapeDtypeStruct((tile, 4 * tile), BF16),
            jax.ShapeDtypeStruct((2, tile // 2, width), F32),
            jax.ShapeDtypeStruct((2, tile // 2, width), BF16),
        ),
        in_specs=[pl.BlockSpec(memory_space=pltpu.SMEM)] + vmem(7),
        out_specs=tuple(vmem(4)),
        scratch_shapes=[
            pltpu.VMEM((2 * tile, width), BF16),
            pltpu.VMEM((2 * tile, width), BF16),
            pltpu.VMEM((2 * tile, width), F32),
        ],
        compiler_params=pltpu.CompilerParams(vmem_limit_bytes=12 << 20),
        cost_estimate=pl.CostEstimate(
            flops=8 * rows * width * width, bytes_accessed=2 << 20, transcendentals=rows * width
        ),
    )(where, near, far, tp1, ct1, w, agg0, gp0)
    got = swap(send, "row", 1, 8)
    summed = keep + got.astype(F32)
    pair_term, gp1 = lax.optimization_barrier((summed[1].astype(BF16), gp1))
    got = swap(pair_term, "col", 2, 4)
    mine = (summed[0] + got.astype(F32)).astype(BF16)
    back, part = pl.pallas_call(
        backward_kernel,
        out_shape=(
            jax.ShapeDtypeStruct((rows, width), BF16),
            jax.ShapeDtypeStruct((rows, width), F32),
        ),
        in_specs=vmem(5),
        out_specs=tuple(vmem(2)),
        compiler_params=pltpu.CompilerParams(vmem_limit_bytes=12 << 20),
        cost_estimate=pl.CostEstimate(
            flops=2 * 256 * 512 * 512 * 2, bytes_accessed=2 << 20, transcendentals=0
        ),
    )(gp0, gp1, adj0, adj1, w)
    got_back = swap(back, "col", 2, 4)
    mine, back = lax.optimization_barrier((mine, back))
    diagonal = swap(mine, "row", 6, 8).astype(F32)
    along = swap(mine, "row", 4, 8).astype(F32)
    across = swap(mine, "row", 2, 8).astype(F32)
    grad_features = (part + got_back.astype(F32)).astype(BF16)
    along, grad_features = lax.optimization_barrier((along, grad_features))
    total = (mine.astype(F32) + across) + (along + diagonal)
    rest = swap(total, "row", 1, 8)
    first = jnp.where(half == 0, total, rest)
    second = jnp.where(half == 0, rest, total)
    grad_weight = jnp.concatenate([first, second], axis=0)
    return (out, grad_features, grad_weight)


def solution(mesh):
    sizes = (mesh.shape["row"], mesh.shape["col"])

    def on_device(*args):
        rows, width = args[0].shape
        tile = args[3].shape[1]
        small = sizes == (8, 4) and rows == tile and width == 4 * tile
        return (four_by_eight if small else any_mesh)(*args)

    return jax.shard_map(
        on_device,
        mesh=mesh,
        in_specs=(
            P(("row", "col"), None),
            P(),
            P(("row", "col"), None),
            P(("row", "col"), None, None),
            P(("row", "col"), None),
            P(("row", "col")),
        ),
        out_specs=(P(("row", "col"), None), P(("row", "col"), None), P("col", None)),
        check_vma=False,
    )
```

```python
import functools
import math

import jax
import jax.numpy as jnp
from jax import lax
from jax.experimental import pallas as pl
from jax.experimental.pallas import tpu as pltpu
from jax.sharding import PartitionSpec as P

F32 = jnp.float32
BF16 = jnp.bfloat16


def tile_range(tile_col, live_mask, first, extent):
    lower = jnp.sum(jnp.where(live_mask & (tile_col < first), 1, 0)).astype(jnp.int32)
    upper = jnp.sum(jnp.where(live_mask & (tile_col < first + extent), 1, 0)).astype(jnp.int32)
    return (lower, upper)


def any_mesh(features, weight, cotangent, tile_blocks, tile_index, tile_count):
    rows, width = features.shape
    tile = tile_blocks.shape[1]
    row_tiles = rows // tile
    slots = tile_blocks.shape[0]
    index = tile_index[0]
    live_mask = jnp.arange(slots, dtype=jnp.int32) < tile_count[0]
    tile_col = index // row_tiles
    tile_row = index % row_tiles
    panels = features.reshape(row_tiles, tile, width)
    piece = lax.all_gather(panels, "col", axis=0, tiled=True)
    lower, upper = tile_range(tile_col, live_mask, jnp.int32(0), piece.shape[0])

    def add_step(slot, acc):
        block = lax.dynamic_index_in_dim(tile_blocks, slot, 0, keepdims=False)
        source = lax.dynamic_index_in_dim(piece, tile_col[slot], 0, keepdims=False)
        product = jnp.dot(block, source, preferred_element_type=F32)
        current = lax.dynamic_index_in_dim(acc, tile_row[slot], 0, keepdims=False)
        return lax.dynamic_update_index_in_dim(acc, current + product, tile_row[slot], 0)

    summed = lax.fori_loop(lower, upper, add_step, panels.astype(F32))
    aggregated = summed.reshape(rows, width).astype(BF16)
    pre_act = jnp.dot(aggregated, weight, preferred_element_type=F32)
    sigmoid_pre = jax.nn.sigmoid(pre_act)
    out_features = (pre_act * sigmoid_pre).astype(BF16)
    grad_pre = (
        cotangent.astype(F32) * sigmoid_pre * (1.0 + pre_act * (1.0 - sigmoid_pre))
    ).astype(BF16)
    node_total = rows * lax.axis_size("row") * lax.axis_size("col")
    local_weight = lax.dot_general(
        aggregated, grad_pre, (((0,), (0,)), ((), ())), preferred_element_type=F32
    ) * (1.0 / math.sqrt(node_total))
    grad_mid = lax.dot_general(
        grad_pre, weight, (((1,), (1,)), ((), ())), preferred_element_type=F32
    ).astype(BF16)
    mid_tiles = grad_mid.reshape(row_tiles, tile, width)
    extent = lax.axis_size("col") * rows
    first = jnp.int32(0) // tile
    tiles_here = extent // tile
    lower, upper = tile_range(tile_col, live_mask, first, tiles_here)

    def spread_step(slot, acc):
        block = lax.dynamic_index_in_dim(tile_blocks, slot, 0, keepdims=False)
        source = lax.dynamic_index_in_dim(mid_tiles, tile_row[slot], 0, keepdims=False)
        product = lax.dot_general(
            block, source, (((0,), (0,)), ((), ())), preferred_element_type=F32
        )
        target = tile_col[slot]
        current = lax.dynamic_index_in_dim(acc, target, 0, keepdims=False)
        return lax.dynamic_update_index_in_dim(acc, current + product, target, 0)

    terms = lax.fori_loop(
        lower, upper, spread_step, jnp.zeros((tiles_here, tile, width), F32)
    )
    gathered_back = lax.psum_scatter(
        terms.reshape(extent, width).astype(BF16), "col", scatter_dimension=0, tiled=True
    ).astype(F32)
    grad_features = (grad_mid.astype(F32) + gathered_back).astype(BF16)
    share = width // lax.axis_size("col")
    total_weight = lax.psum(local_weight, ("row", "col"))
    grad_weight = lax.dynamic_slice_in_dim(total_weight, lax.axis_index("col") * share, share, 0)
    return (out_features, grad_features, grad_weight)


def swap(value, axis, mask, size):
    return lax.ppermute(value, axis, [(i, i ^ mask) for i in range(size)])


def vmem(count):
    return [pl.BlockSpec(memory_space=pltpu.VMEM)] * count


def place(adj, row, tp, own, slots):
    tile = tp.shape[1]
    for t in range(4):
        name = (own ^ t).astype(F32)
        total = jnp.zeros((tile, tile), F32)
        for s in range(slots):
            mark = tp[pl.ds(slots * tile + 16 * s, 16), :][0:1, :].astype(F32)
            block = tp[pl.ds(s * tile, tile), :]
            total = total + jnp.where(mark == name, block.astype(F32), 0.0)
        adj[pl.ds(row, tile), pl.ds(t * tile, tile)] = total.astype(BF16)


def stage_kernel(slots, where, tp, f, ct, w, f_out, ct_out, w_out, adj):
    place(adj, 0, tp, where[0], slots)
    f_out[...] = f[...]
    ct_out[...] = ct[...]
    w_out[...] = w[...]


def activate(adj, near, far, own_rows, ct, w):
    half = near.shape[0]
    summed = own_rows.astype(F32)
    summed = summed + jnp.dot(adj[:, :half], near, preferred_element_type=F32)
    summed = summed + jnp.dot(adj[:, half:], far, preferred_element_type=F32)
    agg = summed.astype(BF16)
    pre = jnp.dot(agg, w, preferred_element_type=F32)
    sig = jax.nn.sigmoid(pre)
    slope = ct.astype(F32) * sig * (1.0 + pre * (1.0 - sig))
    return agg, pre, slope.astype(BF16)


def own_kernel(f1, f2, f3, f0, adj, ct, w, pre, agg, gp, near, far):
    tile = f1.shape[0]
    near[:tile], near[tile:] = f0[...], f1[...]
    far[:tile], far[tile:] = f2[...], f3[...]
    agg[...], pre[...], gp[...] = activate(adj[...], near[...], far[...], f0[...], ct[...], w[...])


def pair_kernel(scale, slots, where, near, far, tp, ct, w, agg0, gp0,
                gp1, adj, keep, send, agg, gp, gw):
    tile = tp.shape[1]
    own, half = where[0], where[1]
    place(adj, 0, tp, own, slots)
    agg[:tile], gp[:tile] = agg0[...], gp0[...]
    agg1, _, slope = activate(adj[...], near[...], far[...], near[tile:], ct[...], w[...])
    agg[tile:], gp[tile:], gp1[...] = agg1, slope, slope
    part = tile // 2
    for b in range(2):
        lane = pl.multiple_of((own ^ (2 * b)) * tile, tile)
        gw[pl.ds(b * tile, tile), :] = lax.dot_general(
            agg[:, pl.ds(lane, tile)], gp[...], (((0,), (0,)), ((), ())),
            preferred_element_type=F32,
        ) * scale
        mine = pl.multiple_of(b * tile + half * part, part)
        other = pl.multiple_of(b * tile + (1 - half) * part, part)
        keep[b] = gw[pl.ds(mine, part), :]
        send[b] = gw[pl.ds(other, part), :].astype(BF16)


def pack_kernel(index, count, blocks, packed):
    slots, tile, _ = blocks.shape
    for s in range(slots):
        packed[pl.ds(s * tile, tile), :] = blocks[s]
        mark = jnp.where(s < count[0], index[0, s], -1).astype(F32)
        packed[pl.ds(slots * tile + 16 * s, 16), :] = jnp.full((16, tile), mark, F32).astype(BF16)


def backward_kernel(gp0, gp1, adj0, adj1, w, back, part):
    tile = gp0.shape[0]
    terms = jnp.zeros((2 * tile, w.shape[0]), F32)
    for b, (gp, adj) in enumerate(((gp0, adj0), (gp1, adj1))):
        mid = lax.dot_general(
            gp[...], w[...], (((1,), (1,)), ((), ())), preferred_element_type=F32
        ).astype(BF16)
        sel = jnp.concatenate([adj[:, :tile], adj[:, 2 * tile : 3 * tile]], axis=1)
        terms = terms + lax.dot_general(
            sel, mid, (((0,), (0,)), ((), ())), preferred_element_type=F32
        )
        if b == 0:
            part[...] = mid.astype(F32)
    back[...] = terms[tile:].astype(BF16)
    part[...] = part[...] + terms[:tile]


def four_by_eight(features, weight, cotangent, tile_blocks, tile_index, tile_count):
    rows, width = features.shape
    slots, tile, _ = tile_blocks.shape
    own = lax.axis_index("col")
    half = lax.axis_index("row") & 1
    where = jnp.stack([own, half]).astype(jnp.int32)
    f3 = swap(features, "col", 3, 4)
    f2 = swap(features, "col", 2, 4)
    f1 = swap(features, "col", 1, 4)
    ct1 = swap(cotangent, "col", 1, 4)
    tp0 = pl.pallas_call(
        pack_kernel,
        out_shape=jax.ShapeDtypeStruct((slots * (tile + 16), tile), BF16),
        in_specs=[pl.BlockSpec(memory_space=pltpu.SMEM)] * 2 + vmem(1),
        out_specs=vmem(1)[0],
        compiler_params=pltpu.CompilerParams(vmem_limit_bytes=2 << 20),
    )(tile_index, tile_count, tile_blocks)
    tp1 = swap(tp0, "col", 1, 4)
    f0, ct0, w, adj0 = pl.pallas_call(
        functools.partial(stage_kernel, slots),
        out_shape=(
            jax.ShapeDtypeStruct((rows, width), BF16),
            jax.ShapeDtypeStruct((rows, width), BF16),
            jax.ShapeDtypeStruct((width, width), BF16),
            jax.ShapeDtypeStruct((tile, 4 * tile), BF16),
        ),
        in_specs=[pl.BlockSpec(memory_space=pltpu.SMEM)] + vmem(4),
        out_specs=tuple(vmem(4)),
        compiler_params=pltpu.CompilerParams(vmem_limit_bytes=8 << 20),
    )(where, tp0, features, cotangent, weight)
    scale = 1.0 / math.sqrt(rows * lax.axis_size("row") * lax.axis_size("col"))
    block = jax.ShapeDtypeStruct((rows, width), BF16)
    double = jax.ShapeDtypeStruct((2 * rows, width), BF16)
    pre, agg0, gp0, near, far = pl.pallas_call(
        own_kernel,
        out_shape=(jax.ShapeDtypeStruct((rows, width), F32), block, block, double, double),
        in_specs=vmem(7),
        out_specs=tuple(vmem(5)),
        compiler_params=pltpu.CompilerParams(vmem_limit_bytes=8 << 20),
        cost_estimate=pl.CostEstimate(
            flops=4 * rows * width * width, bytes_accessed=1 << 20, transcendentals=rows * width
        ),
    )(f1, f2, f3, f0, adj0, ct0, w)
    gp1, adj1, keep, send = pl.pallas_call(
        functools.partial(pair_kernel, scale, slots),
        out_shape=(
            block,
            jax.ShapeDtypeStruct((tile, 4 * tile), BF16),
            jax.ShapeDtypeStruct((2, tile // 2, width), F32),
            jax.ShapeDtypeStruct((2, tile // 2, width), BF16),
        ),
        in_specs=[pl.BlockSpec(memory_space=pltpu.SMEM)] + vmem(7),
        out_specs=tuple(vmem(4)),
        scratch_shapes=[
            pltpu.VMEM((2 * tile, width), BF16),
            pltpu.VMEM((2 * tile, width), BF16),
            pltpu.VMEM((2 * tile, width), F32),
        ],
        compiler_params=pltpu.CompilerParams(vmem_limit_bytes=12 << 20),
        cost_estimate=pl.CostEstimate(
            flops=8 * rows * width * width, bytes_accessed=2 << 20, transcendentals=rows * width
        ),
    )(where, near, far, tp1, ct1, w, agg0, gp0)
    got = swap(send, "row", 1, 8)
    summed = keep + got.astype(F32)
    pair_term, gp1 = lax.optimization_barrier((summed[1].astype(BF16), gp1))
    got = swap(pair_term, "col", 2, 4)
    mine = (summed[0] + got.astype(F32)).astype(BF16)
    back, part = pl.pallas_call(
        backward_kernel,
        out_shape=(
            jax.ShapeDtypeStruct((rows, width), BF16),
            jax.ShapeDtypeStruct((rows, width), F32),
        ),
        in_specs=vmem(5),
        out_specs=tuple(vmem(2)),
        compiler_params=pltpu.CompilerParams(vmem_limit_bytes=12 << 20),
        cost_estimate=pl.CostEstimate(
            flops=2 * 256 * 512 * 512 * 2, bytes_accessed=2 << 20, transcendentals=0
        ),
    )(gp0, gp1, adj0, adj1, w)
    odd = lax.ppermute(back, "col", [(1, 3), (3, 1)])
    even = lax.ppermute(back, "col", [(0, 2), (2, 0)])
    mine, back = lax.optimization_barrier((mine, back))
    diagonal = swap(mine, "row", 6, 8).astype(F32)
    along = swap(mine, "row", 4, 8).astype(F32)
    across = swap(mine, "row", 2, 8).astype(F32)
    grad_features = (part + (odd.astype(F32) + even.astype(F32))).astype(BF16)
    out = (pre * jax.nn.sigmoid(pre)).astype(BF16)
    along, grad_features = lax.optimization_barrier((along, grad_features))
    total = (mine.astype(F32) + across) + (along + diagonal)
    rest = swap(total, "row", 1, 8)
    first = jnp.where(half == 0, total, rest)
    second = jnp.where(half == 0, rest, total)
    grad_weight = jnp.concatenate([first, second], axis=0)
    return (out, grad_features, grad_weight)


def solution(mesh):
    sizes = (mesh.shape["row"], mesh.shape["col"])

    def on_device(*args):
        rows, width = args[0].shape
        tile = args[3].shape[1]
        small = sizes == (8, 4) and rows == tile and width == 4 * tile
        return (four_by_eight if small else any_mesh)(*args)

    return jax.shard_map(
        on_device,
        mesh=mesh,
        in_specs=(
            P(("row", "col"), None),
            P(),
            P(("row", "col"), None),
            P(("row", "col"), None, None),
            P(("row", "col"), None),
            P(("row", "col")),
        ),
        out_specs=(P(("row", "col"), None), P(("row", "col"), None), P("col", None)),
        check_vma=False,
    )
```

```python
import functools
import math

import jax
import jax.numpy as jnp
from jax import lax
from jax.experimental import pallas as pl
from jax.experimental.pallas import tpu as pltpu
from jax.sharding import PartitionSpec as P

F32 = jnp.float32
BF16 = jnp.bfloat16


def tile_range(tile_col, live_mask, first, extent):
    lower = jnp.sum(jnp.where(live_mask & (tile_col < first), 1, 0)).astype(jnp.int32)
    upper = jnp.sum(jnp.where(live_mask & (tile_col < first + extent), 1, 0)).astype(jnp.int32)
    return (lower, upper)


def any_mesh(features, weight, cotangent, tile_blocks, tile_index, tile_count):
    rows, width = features.shape
    tile = tile_blocks.shape[1]
    row_tiles = rows // tile
    slots = tile_blocks.shape[0]
    index = tile_index[0]
    live_mask = jnp.arange(slots, dtype=jnp.int32) < tile_count[0]
    tile_col = index // row_tiles
    tile_row = index % row_tiles
    panels = features.reshape(row_tiles, tile, width)
    piece = lax.all_gather(panels, "col", axis=0, tiled=True)
    lower, upper = tile_range(tile_col, live_mask, jnp.int32(0), piece.shape[0])

    def add_step(slot, acc):
        block = lax.dynamic_index_in_dim(tile_blocks, slot, 0, keepdims=False)
        source = lax.dynamic_index_in_dim(piece, tile_col[slot], 0, keepdims=False)
        product = jnp.dot(block, source, preferred_element_type=F32)
        current = lax.dynamic_index_in_dim(acc, tile_row[slot], 0, keepdims=False)
        return lax.dynamic_update_index_in_dim(acc, current + product, tile_row[slot], 0)

    summed = lax.fori_loop(lower, upper, add_step, panels.astype(F32))
    aggregated = summed.reshape(rows, width).astype(BF16)
    pre_act = jnp.dot(aggregated, weight, preferred_element_type=F32)
    sigmoid_pre = jax.nn.sigmoid(pre_act)
    out_features = (pre_act * sigmoid_pre).astype(BF16)
    grad_pre = (
        cotangent.astype(F32) * sigmoid_pre * (1.0 + pre_act * (1.0 - sigmoid_pre))
    ).astype(BF16)
    node_total = rows * lax.axis_size("row") * lax.axis_size("col")
    local_weight = lax.dot_general(
        aggregated, grad_pre, (((0,), (0,)), ((), ())), preferred_element_type=F32
    ) * (1.0 / math.sqrt(node_total))
    grad_mid = lax.dot_general(
        grad_pre, weight, (((1,), (1,)), ((), ())), preferred_element_type=F32
    ).astype(BF16)
    mid_tiles = grad_mid.reshape(row_tiles, tile, width)
    extent = lax.axis_size("col") * rows
    first = jnp.int32(0) // tile
    tiles_here = extent // tile
    lower, upper = tile_range(tile_col, live_mask, first, tiles_here)

    def spread_step(slot, acc):
        block = lax.dynamic_index_in_dim(tile_blocks, slot, 0, keepdims=False)
        source = lax.dynamic_index_in_dim(mid_tiles, tile_row[slot], 0, keepdims=False)
        product = lax.dot_general(
            block, source, (((0,), (0,)), ((), ())), preferred_element_type=F32
        )
        target = tile_col[slot]
        current = lax.dynamic_index_in_dim(acc, target, 0, keepdims=False)
        return lax.dynamic_update_index_in_dim(acc, current + product, target, 0)

    terms = lax.fori_loop(
        lower, upper, spread_step, jnp.zeros((tiles_here, tile, width), F32)
    )
    gathered_back = lax.psum_scatter(
        terms.reshape(extent, width).astype(BF16), "col", scatter_dimension=0, tiled=True
    ).astype(F32)
    grad_features = (grad_mid.astype(F32) + gathered_back).astype(BF16)
    share = width // lax.axis_size("col")
    total_weight = lax.psum(local_weight, ("row", "col"))
    grad_weight = lax.dynamic_slice_in_dim(total_weight, lax.axis_index("col") * share, share, 0)
    return (out_features, grad_features, grad_weight)


def swap(value, axis, mask, size):
    return lax.ppermute(value, axis, [(i, i ^ mask) for i in range(size)])


def vmem(count):
    return [pl.BlockSpec(memory_space=pltpu.VMEM)] * count


def place(adj, row, tp, own, slots):
    tile = tp.shape[1]
    for t in range(4):
        name = (own ^ t).astype(F32)
        total = jnp.zeros((tile, tile), F32)
        for s in range(slots):
            mark = tp[pl.ds(slots * tile + 16 * s, 16), :][0:1, :].astype(F32)
            block = tp[pl.ds(s * tile, tile), :]
            total = total + jnp.where(mark == name, block.astype(F32), 0.0)
        adj[pl.ds(row, tile), pl.ds(t * tile, tile)] = total.astype(BF16)


def stage_kernel(slots, where, tp, f, ct, w, f_out, ct_out, w_out, adj):
    place(adj, 0, tp, where[0], slots)
    f_out[...] = f[...]
    ct_out[...] = ct[...]
    w_out[...] = w[...]


def activate(adj, near, far, own_rows, ct, w):
    half = near.shape[0]
    summed = own_rows.astype(F32)
    summed = summed + jnp.dot(adj[:, :half], near, preferred_element_type=F32)
    summed = summed + jnp.dot(adj[:, half:], far, preferred_element_type=F32)
    agg = summed.astype(BF16)
    pre = jnp.dot(agg, w, preferred_element_type=F32)
    sig = jax.nn.sigmoid(pre)
    slope = ct.astype(F32) * sig * (1.0 + pre * (1.0 - sig))
    return agg, pre, slope.astype(BF16)


def own_kernel(f1, f2, f3, f0, adj, ct, w, pre, agg, gp, near, far):
    tile = f1.shape[0]
    near[:tile], near[tile:] = f0[...], f1[...]
    far[:tile], far[tile:] = f2[...], f3[...]
    agg[...], pre[...], gp[...] = activate(adj[...], near[...], far[...], f0[...], ct[...], w[...])


def pair_kernel(scale, slots, where, near, far, tp, ct, w, agg0, gp0,
                gp1, adj, keep, send, agg, gp, gw):
    tile = tp.shape[1]
    own, half = where[0], where[1]
    place(adj, 0, tp, own, slots)
    agg[:tile], gp[:tile] = agg0[...], gp0[...]
    agg1, _, slope = activate(adj[...], near[...], far[...], near[tile:], ct[...], w[...])
    agg[tile:], gp[tile:], gp1[...] = agg1, slope, slope
    part = tile // 2
    for b in range(2):
        lane = pl.multiple_of((own ^ (2 * b)) * tile, tile)
        gw[pl.ds(b * tile, tile), :] = lax.dot_general(
            agg[:, pl.ds(lane, tile)], gp[...], (((0,), (0,)), ((), ())),
            preferred_element_type=F32,
        ) * scale
        mine = pl.multiple_of(b * tile + half * part, part)
        other = pl.multiple_of(b * tile + (1 - half) * part, part)
        keep[b] = gw[pl.ds(mine, part), :]
        send[b] = gw[pl.ds(other, part), :].astype(BF16)


def pack_kernel(index, count, blocks, packed):
    slots, tile, _ = blocks.shape
    for s in range(slots):
        packed[pl.ds(s * tile, tile), :] = blocks[s]
        mark = jnp.where(s < count[0], index[0, s], -1).astype(F32)
        packed[pl.ds(slots * tile + 16 * s, 16), :] = jnp.full((16, tile), mark, F32).astype(BF16)


def backward_kernel(gp0, gp1, adj0, adj1, w, back, part):
    tile = gp0.shape[0]
    terms = jnp.zeros((2 * tile, w.shape[0]), F32)
    for b, (gp, adj) in enumerate(((gp0, adj0), (gp1, adj1))):
        mid = lax.dot_general(
            gp[...], w[...], (((1,), (1,)), ((), ())), preferred_element_type=F32
        ).astype(BF16)
        sel = jnp.concatenate([adj[:, :tile], adj[:, 2 * tile : 3 * tile]], axis=1)
        terms = terms + lax.dot_general(
            sel, mid, (((0,), (0,)), ((), ())), preferred_element_type=F32
        )
        if b == 0:
            part[...] = mid.astype(F32)
    back[...] = terms[tile:].astype(BF16)
    part[...] = part[...] + terms[:tile]


def four_by_eight(features, weight, cotangent, tile_blocks, tile_index, tile_count):
    rows, width = features.shape
    slots, tile, _ = tile_blocks.shape
    own = lax.axis_index("col")
    half = lax.axis_index("row") & 1
    where = jnp.stack([own, half]).astype(jnp.int32)
    f3 = swap(features, "col", 3, 4)
    f2 = swap(features, "col", 2, 4)
    f1 = swap(features, "col", 1, 4)
    ct1 = swap(cotangent, "col", 1, 4)
    tp0 = pl.pallas_call(
        pack_kernel,
        out_shape=jax.ShapeDtypeStruct((slots * (tile + 16), tile), BF16),
        in_specs=[pl.BlockSpec(memory_space=pltpu.SMEM)] * 2 + vmem(1),
        out_specs=vmem(1)[0],
        compiler_params=pltpu.CompilerParams(vmem_limit_bytes=2 << 20),
    )(tile_index, tile_count, tile_blocks)
    tp1 = swap(tp0, "col", 1, 4)
    f0, ct0, w, adj0 = pl.pallas_call(
        functools.partial(stage_kernel, slots),
        out_shape=(
            jax.ShapeDtypeStruct((rows, width), BF16),
            jax.ShapeDtypeStruct((rows, width), BF16),
            jax.ShapeDtypeStruct((width, width), BF16),
            jax.ShapeDtypeStruct((tile, 4 * tile), BF16),
        ),
        in_specs=[pl.BlockSpec(memory_space=pltpu.SMEM)] + vmem(4),
        out_specs=tuple(vmem(4)),
        compiler_params=pltpu.CompilerParams(vmem_limit_bytes=8 << 20),
    )(where, tp0, features, cotangent, weight)
    scale = 1.0 / math.sqrt(rows * lax.axis_size("row") * lax.axis_size("col"))
    block = jax.ShapeDtypeStruct((rows, width), BF16)
    double = jax.ShapeDtypeStruct((2 * rows, width), BF16)
    pre, agg0, gp0, near, far = pl.pallas_call(
        own_kernel,
        out_shape=(jax.ShapeDtypeStruct((rows, width), F32), block, block, double, double),
        in_specs=vmem(7),
        out_specs=tuple(vmem(5)),
        compiler_params=pltpu.CompilerParams(vmem_limit_bytes=8 << 20),
        cost_estimate=pl.CostEstimate(
            flops=4 * rows * width * width, bytes_accessed=1 << 20, transcendentals=rows * width
        ),
    )(f1, f2, f3, f0, adj0, ct0, w)
    gp1, adj1, keep, send = pl.pallas_call(
        functools.partial(pair_kernel, scale, slots),
        out_shape=(
            block,
            jax.ShapeDtypeStruct((tile, 4 * tile), BF16),
            jax.ShapeDtypeStruct((2, tile // 2, width), F32),
            jax.ShapeDtypeStruct((2, tile // 2, width), BF16),
        ),
        in_specs=[pl.BlockSpec(memory_space=pltpu.SMEM)] + vmem(7),
        out_specs=tuple(vmem(4)),
        scratch_shapes=[
            pltpu.VMEM((2 * tile, width), BF16),
            pltpu.VMEM((2 * tile, width), BF16),
            pltpu.VMEM((2 * tile, width), F32),
        ],
        compiler_params=pltpu.CompilerParams(vmem_limit_bytes=12 << 20),
        cost_estimate=pl.CostEstimate(
            flops=8 * rows * width * width, bytes_accessed=2 << 20, transcendentals=rows * width
        ),
    )(where, near, far, tp1, ct1, w, agg0, gp0)
    got = swap(send, "row", 1, 8)
    summed = keep + got.astype(F32)
    pair_term, gp1 = lax.optimization_barrier((summed[1].astype(BF16), gp1))
    got = swap(pair_term, "col", 2, 4)
    mine = (summed[0] + got.astype(F32)).astype(BF16)
    back, part = pl.pallas_call(
        backward_kernel,
        out_shape=(
            jax.ShapeDtypeStruct((rows, width), BF16),
            jax.ShapeDtypeStruct((rows, width), F32),
        ),
        in_specs=vmem(5),
        out_specs=tuple(vmem(2)),
        compiler_params=pltpu.CompilerParams(vmem_limit_bytes=12 << 20),
        cost_estimate=pl.CostEstimate(
            flops=2 * 256 * 512 * 512 * 2, bytes_accessed=2 << 20, transcendentals=0
        ),
    )(gp0, gp1, adj0, adj1, w)
    odd = lax.ppermute(back, "col", [(1, 3), (3, 1)])
    even = lax.ppermute(back, "col", [(0, 2), (2, 0)])
    mine, back = lax.optimization_barrier((mine, back))
    diagonal = swap(mine, "row", 6, 8).astype(F32)
    along = swap(mine, "row", 4, 8).astype(F32)
    across = swap(mine, "row", 2, 8).astype(F32)
    along, even, odd = lax.optimization_barrier((along, even, odd))
    out = (pre * jax.nn.sigmoid(pre)).astype(BF16)
    total = (mine.astype(F32) + across) + (along + diagonal)
    rest = swap(total, "row", 1, 8)
    grad_features = (part + (odd.astype(F32) + even.astype(F32))).astype(BF16)
    first = jnp.where(half == 0, total, rest)
    second = jnp.where(half == 0, rest, total)
    grad_weight = jnp.concatenate([first, second], axis=0)
    return (out, grad_features, grad_weight)


def solution(mesh):
    sizes = (mesh.shape["row"], mesh.shape["col"])

    def on_device(*args):
        rows, width = args[0].shape
        tile = args[3].shape[1]
        small = sizes == (8, 4) and rows == tile and width == 4 * tile
        return (four_by_eight if small else any_mesh)(*args)

    return jax.shard_map(
        on_device,
        mesh=mesh,
        in_specs=(
            P(("row", "col"), None),
            P(),
            P(("row", "col"), None),
            P(("row", "col"), None, None),
            P(("row", "col"), None),
            P(("row", "col")),
        ),
        out_specs=(P(("row", "col"), None), P(("row", "col"), None), P("col", None)),
        check_vma=False,
    )
```

```python
import functools
import math

import jax
import jax.numpy as jnp
from jax import lax
from jax.experimental import pallas as pl
from jax.experimental.pallas import tpu as pltpu
from jax.sharding import PartitionSpec as P

F32 = jnp.float32
BF16 = jnp.bfloat16


def tile_range(tile_col, live_mask, first, extent):
    lower = jnp.sum(jnp.where(live_mask & (tile_col < first), 1, 0)).astype(jnp.int32)
    upper = jnp.sum(jnp.where(live_mask & (tile_col < first + extent), 1, 0)).astype(jnp.int32)
    return (lower, upper)


def any_mesh(features, weight, cotangent, tile_blocks, tile_index, tile_count):
    rows, width = features.shape
    tile = tile_blocks.shape[1]
    row_tiles = rows // tile
    slots = tile_blocks.shape[0]
    index = tile_index[0]
    live_mask = jnp.arange(slots, dtype=jnp.int32) < tile_count[0]
    tile_col = index // row_tiles
    tile_row = index % row_tiles
    panels = features.reshape(row_tiles, tile, width)
    piece = lax.all_gather(panels, "col", axis=0, tiled=True)
    lower, upper = tile_range(tile_col, live_mask, jnp.int32(0), piece.shape[0])

    def add_step(slot, acc):
        block = lax.dynamic_index_in_dim(tile_blocks, slot, 0, keepdims=False)
        source = lax.dynamic_index_in_dim(piece, tile_col[slot], 0, keepdims=False)
        product = jnp.dot(block, source, preferred_element_type=F32)
        current = lax.dynamic_index_in_dim(acc, tile_row[slot], 0, keepdims=False)
        return lax.dynamic_update_index_in_dim(acc, current + product, tile_row[slot], 0)

    summed = lax.fori_loop(lower, upper, add_step, panels.astype(F32))
    aggregated = summed.reshape(rows, width).astype(BF16)
    pre_act = jnp.dot(aggregated, weight, preferred_element_type=F32)
    sigmoid_pre = jax.nn.sigmoid(pre_act)
    out_features = (pre_act * sigmoid_pre).astype(BF16)
    grad_pre = (
        cotangent.astype(F32) * sigmoid_pre * (1.0 + pre_act * (1.0 - sigmoid_pre))
    ).astype(BF16)
    node_total = rows * lax.axis_size("row") * lax.axis_size("col")
    local_weight = lax.dot_general(
        aggregated, grad_pre, (((0,), (0,)), ((), ())), preferred_element_type=F32
    ) * (1.0 / math.sqrt(node_total))
    grad_mid = lax.dot_general(
        grad_pre, weight, (((1,), (1,)), ((), ())), preferred_element_type=F32
    ).astype(BF16)
    mid_tiles = grad_mid.reshape(row_tiles, tile, width)
    extent = lax.axis_size("col") * rows
    first = jnp.int32(0) // tile
    tiles_here = extent // tile
    lower, upper = tile_range(tile_col, live_mask, first, tiles_here)

    def spread_step(slot, acc):
        block = lax.dynamic_index_in_dim(tile_blocks, slot, 0, keepdims=False)
        source = lax.dynamic_index_in_dim(mid_tiles, tile_row[slot], 0, keepdims=False)
        product = lax.dot_general(
            block, source, (((0,), (0,)), ((), ())), preferred_element_type=F32
        )
        target = tile_col[slot]
        current = lax.dynamic_index_in_dim(acc, target, 0, keepdims=False)
        return lax.dynamic_update_index_in_dim(acc, current + product, target, 0)

    terms = lax.fori_loop(
        lower, upper, spread_step, jnp.zeros((tiles_here, tile, width), F32)
    )
    gathered_back = lax.psum_scatter(
        terms.reshape(extent, width).astype(BF16), "col", scatter_dimension=0, tiled=True
    ).astype(F32)
    grad_features = (grad_mid.astype(F32) + gathered_back).astype(BF16)
    share = width // lax.axis_size("col")
    total_weight = lax.psum(local_weight, ("row", "col"))
    grad_weight = lax.dynamic_slice_in_dim(total_weight, lax.axis_index("col") * share, share, 0)
    return (out_features, grad_features, grad_weight)


def swap(value, axis, mask, size):
    return lax.ppermute(value, axis, [(i, i ^ mask) for i in range(size)])


def vmem(count):
    return [pl.BlockSpec(memory_space=pltpu.VMEM)] * count


def place(adj, row, tp, own, slots):
    tile = tp.shape[1]
    for t in range(4):
        name = (own ^ t).astype(F32)
        total = jnp.zeros((tile, tile), F32)
        for s in range(slots):
            mark = tp[pl.ds(slots * tile + 16 * s, 16), :][0:1, :].astype(F32)
            block = tp[pl.ds(s * tile, tile), :]
            total = total + jnp.where(mark == name, block.astype(F32), 0.0)
        adj[pl.ds(row, tile), pl.ds(t * tile, tile)] = total.astype(BF16)


def stage_kernel(slots, where, tp, f, ct, w, f_out, ct_out, w_out, adj):
    place(adj, 0, tp, where[0], slots)
    f_out[...] = f[...]
    ct_out[...] = ct[...]
    w_out[...] = w[...]


def activate(adj, near, far, own_rows, ct, w):
    half = near.shape[0]
    summed = own_rows.astype(F32)
    summed = summed + jnp.dot(adj[:, :half], near, preferred_element_type=F32)
    summed = summed + jnp.dot(adj[:, half:], far, preferred_element_type=F32)
    agg = summed.astype(BF16)
    pre = jnp.dot(agg, w, preferred_element_type=F32)
    sig = jax.nn.sigmoid(pre)
    slope = ct.astype(F32) * sig * (1.0 + pre * (1.0 - sig))
    return agg, pre, slope.astype(BF16)


def own_kernel(f1, f2, f3, f0, adj, ct, w, pre, agg, gp, near, far):
    tile = f1.shape[0]
    near[:tile], near[tile:] = f0[...], f1[...]
    far[:tile], far[tile:] = f2[...], f3[...]
    agg[...], pre[...], gp[...] = activate(adj[...], near[...], far[...], f0[...], ct[...], w[...])


def pair_kernel(scale, slots, where, near, far, tp, ct, w, agg0, gp0,
                gp1, adj, keep, send, agg, gp, gw):
    tile = tp.shape[1]
    own, half = where[0], where[1]
    place(adj, 0, tp, own, slots)
    agg[:tile], gp[:tile] = agg0[...], gp0[...]
    agg1, _, slope = activate(adj[...], near[...], far[...], near[tile:], ct[...], w[...])
    agg[tile:], gp[tile:], gp1[...] = agg1, slope, slope
    part = tile // 2
    for b in range(2):
        lane = pl.multiple_of((own ^ (2 * b)) * tile, tile)
        gw[pl.ds(b * tile, tile), :] = lax.dot_general(
            agg[:, pl.ds(lane, tile)], gp[...], (((0,), (0,)), ((), ())),
            preferred_element_type=F32,
        ) * scale
        mine = pl.multiple_of(b * tile + half * part, part)
        other = pl.multiple_of(b * tile + (1 - half) * part, part)
        keep[b] = gw[pl.ds(mine, part), :]
        send[b] = gw[pl.ds(other, part), :].astype(BF16)


def pack_kernel(index, count, blocks, packed):
    slots, tile, _ = blocks.shape
    for s in range(slots):
        packed[pl.ds(s * tile, tile), :] = blocks[s]
        mark = jnp.where(s < count[0], index[0, s], -1).astype(F32)
        packed[pl.ds(slots * tile + 16 * s, 16), :] = jnp.full((16, tile), mark, F32).astype(BF16)


def backward_kernel(gp0, gp1, adj0, adj1, w, back, part):
    tile = gp0.shape[0]
    terms = jnp.zeros((2 * tile, w.shape[0]), F32)
    for b, (gp, adj) in enumerate(((gp0, adj0), (gp1, adj1))):
        mid = lax.dot_general(
            gp[...], w[...], (((1,), (1,)), ((), ())), preferred_element_type=F32
        ).astype(BF16)
        sel = jnp.concatenate([adj[:, :tile], adj[:, 2 * tile : 3 * tile]], axis=1)
        terms = terms + lax.dot_general(
            sel, mid, (((0,), (0,)), ((), ())), preferred_element_type=F32
        )
        if b == 0:
            part[...] = mid.astype(F32)
    back[...] = terms[tile:].astype(BF16)
    part[...] = part[...] + terms[:tile]


def four_by_eight(features, weight, cotangent, tile_blocks, tile_index, tile_count):
    rows, width = features.shape
    slots, tile, _ = tile_blocks.shape
    own = lax.axis_index("col")
    half = lax.axis_index("row") & 1
    where = jnp.stack([own, half]).astype(jnp.int32)
    f3 = swap(features, "col", 3, 4)
    f2 = swap(features, "col", 2, 4)
    f1 = swap(features, "col", 1, 4)
    ct1 = swap(cotangent, "col", 1, 4)
    tp0 = pl.pallas_call(
        pack_kernel,
        out_shape=jax.ShapeDtypeStruct((slots * (tile + 16), tile), BF16),
        in_specs=[pl.BlockSpec(memory_space=pltpu.SMEM)] * 2 + vmem(1),
        out_specs=vmem(1)[0],
        compiler_params=pltpu.CompilerParams(vmem_limit_bytes=2 << 20),
    )(tile_index, tile_count, tile_blocks)
    tp1 = swap(tp0, "col", 1, 4)
    f0, ct0, w, adj0 = pl.pallas_call(
        functools.partial(stage_kernel, slots),
        out_shape=(
            jax.ShapeDtypeStruct((rows, width), BF16),
            jax.ShapeDtypeStruct((rows, width), BF16),
            jax.ShapeDtypeStruct((width, width), BF16),
            jax.ShapeDtypeStruct((tile, 4 * tile), BF16),
        ),
        in_specs=[pl.BlockSpec(memory_space=pltpu.SMEM)] + vmem(4),
        out_specs=tuple(vmem(4)),
        compiler_params=pltpu.CompilerParams(vmem_limit_bytes=8 << 20),
    )(where, tp0, features, cotangent, weight)
    scale = 1.0 / math.sqrt(rows * lax.axis_size("row") * lax.axis_size("col"))
    block = jax.ShapeDtypeStruct((rows, width), BF16)
    double = jax.ShapeDtypeStruct((2 * rows, width), BF16)
    pre, agg0, gp0, near, far = pl.pallas_call(
        own_kernel,
        out_shape=(jax.ShapeDtypeStruct((rows, width), F32), block, block, double, double),
        in_specs=vmem(7),
        out_specs=tuple(vmem(5)),
        compiler_params=pltpu.CompilerParams(vmem_limit_bytes=8 << 20),
        cost_estimate=pl.CostEstimate(
            flops=4 * rows * width * width, bytes_accessed=1 << 20, transcendentals=rows * width
        ),
    )(f1, f2, f3, f0, adj0, ct0, w)
    gp1, adj1, keep, send = pl.pallas_call(
        functools.partial(pair_kernel, scale, slots),
        out_shape=(
            block,
            jax.ShapeDtypeStruct((tile, 4 * tile), BF16),
            jax.ShapeDtypeStruct((2, tile // 2, width), F32),
            jax.ShapeDtypeStruct((2, tile // 2, width), BF16),
        ),
        in_specs=[pl.BlockSpec(memory_space=pltpu.SMEM)] + vmem(7),
        out_specs=tuple(vmem(4)),
        scratch_shapes=[
            pltpu.VMEM((2 * tile, width), BF16),
            pltpu.VMEM((2 * tile, width), BF16),
            pltpu.VMEM((2 * tile, width), F32),
        ],
        compiler_params=pltpu.CompilerParams(vmem_limit_bytes=12 << 20),
        cost_estimate=pl.CostEstimate(
            flops=8 * rows * width * width, bytes_accessed=2 << 20, transcendentals=rows * width
        ),
    )(where, near, far, tp1, ct1, w, agg0, gp0)
    got = swap(send, "row", 1, 8)
    summed = keep + got.astype(F32)
    pair_term, gp1 = lax.optimization_barrier((summed[1].astype(BF16), gp1))
    got = swap(pair_term, "col", 2, 4)
    mine = (summed[0] + got.astype(F32)).astype(BF16)
    back, part = pl.pallas_call(
        backward_kernel,
        out_shape=(
            jax.ShapeDtypeStruct((rows, width), BF16),
            jax.ShapeDtypeStruct((rows, width), F32),
        ),
        in_specs=vmem(5),
        out_specs=tuple(vmem(2)),
        compiler_params=pltpu.CompilerParams(vmem_limit_bytes=12 << 20),
        cost_estimate=pl.CostEstimate(
            flops=2 * 256 * 512 * 512 * 2, bytes_accessed=2 << 20, transcendentals=0
        ),
    )(gp0, gp1, adj0, adj1, w)
    odd = lax.ppermute(back, "col", [(1, 3), (3, 1)])
    even = lax.ppermute(back, "col", [(0, 2), (2, 0)])
    mine, back = lax.optimization_barrier((mine, back))
    diagonal = swap(mine, "row", 6, 8).astype(F32)
    along = swap(mine, "row", 4, 8).astype(F32)
    across = swap(mine, "row", 2, 8).astype(F32)
    along, even, odd = lax.optimization_barrier((along, even, odd))
    out = (pre * jax.nn.sigmoid(pre)).astype(BF16)
    total = (mine.astype(F32) + across) + (along + diagonal)
    total = total.astype(BF16)
    rest = swap(total, "row", 1, 8)
    grad_features = (part + (odd.astype(F32) + even.astype(F32))).astype(BF16)
    first = jnp.where(half == 0, total, rest)
    second = jnp.where(half == 0, rest, total)
    grad_weight = jnp.concatenate([first, second], axis=0).astype(F32)
    return (out, grad_features, grad_weight)


def solution(mesh):
    sizes = (mesh.shape["row"], mesh.shape["col"])

    def on_device(*args):
        rows, width = args[0].shape
        tile = args[3].shape[1]
        small = sizes == (8, 4) and rows == tile and width == 4 * tile
        return (four_by_eight if small else any_mesh)(*args)

    return jax.shard_map(
        on_device,
        mesh=mesh,
        in_specs=(
            P(("row", "col"), None),
            P(),
            P(("row", "col"), None),
            P(("row", "col"), None, None),
            P(("row", "col"), None),
            P(("row", "col")),
        ),
        out_specs=(P(("row", "col"), None), P(("row", "col"), None), P("col", None)),
        check_vma=False,
    )
```

```python
import functools
import math

import jax
import jax.numpy as jnp
from jax import lax
from jax.experimental import pallas as pl
from jax.experimental.pallas import tpu as pltpu
from jax.sharding import PartitionSpec as P

F32 = jnp.float32
BF16 = jnp.bfloat16


def tile_range(tile_col, live_mask, first, extent):
    lower = jnp.sum(jnp.where(live_mask & (tile_col < first), 1, 0)).astype(jnp.int32)
    upper = jnp.sum(jnp.where(live_mask & (tile_col < first + extent), 1, 0)).astype(jnp.int32)
    return (lower, upper)


def any_mesh(features, weight, cotangent, tile_blocks, tile_index, tile_count):
    rows, width = features.shape
    tile = tile_blocks.shape[1]
    row_tiles = rows // tile
    slots = tile_blocks.shape[0]
    index = tile_index[0]
    live_mask = jnp.arange(slots, dtype=jnp.int32) < tile_count[0]
    tile_col = index // row_tiles
    tile_row = index % row_tiles
    panels = features.reshape(row_tiles, tile, width)
    piece = lax.all_gather(panels, "col", axis=0, tiled=True)
    lower, upper = tile_range(tile_col, live_mask, jnp.int32(0), piece.shape[0])

    def add_step(slot, acc):
        block = lax.dynamic_index_in_dim(tile_blocks, slot, 0, keepdims=False)
        source = lax.dynamic_index_in_dim(piece, tile_col[slot], 0, keepdims=False)
        product = jnp.dot(block, source, preferred_element_type=F32)
        current = lax.dynamic_index_in_dim(acc, tile_row[slot], 0, keepdims=False)
        return lax.dynamic_update_index_in_dim(acc, current + product, tile_row[slot], 0)

    summed = lax.fori_loop(lower, upper, add_step, panels.astype(F32))
    aggregated = summed.reshape(rows, width).astype(BF16)
    pre_act = jnp.dot(aggregated, weight, preferred_element_type=F32)
    sigmoid_pre = jax.nn.sigmoid(pre_act)
    out_features = (pre_act * sigmoid_pre).astype(BF16)
    grad_pre = (
        cotangent.astype(F32) * sigmoid_pre * (1.0 + pre_act * (1.0 - sigmoid_pre))
    ).astype(BF16)
    node_total = rows * lax.axis_size("row") * lax.axis_size("col")
    local_weight = lax.dot_general(
        aggregated, grad_pre, (((0,), (0,)), ((), ())), preferred_element_type=F32
    ) * (1.0 / math.sqrt(node_total))
    grad_mid = lax.dot_general(
        grad_pre, weight, (((1,), (1,)), ((), ())), preferred_element_type=F32
    ).astype(BF16)
    mid_tiles = grad_mid.reshape(row_tiles, tile, width)
    extent = lax.axis_size("col") * rows
    first = jnp.int32(0) // tile
    tiles_here = extent // tile
    lower, upper = tile_range(tile_col, live_mask, first, tiles_here)

    def spread_step(slot, acc):
        block = lax.dynamic_index_in_dim(tile_blocks, slot, 0, keepdims=False)
        source = lax.dynamic_index_in_dim(mid_tiles, tile_row[slot], 0, keepdims=False)
        product = lax.dot_general(
            block, source, (((0,), (0,)), ((), ())), preferred_element_type=F32
        )
        target = tile_col[slot]
        current = lax.dynamic_index_in_dim(acc, target, 0, keepdims=False)
        return lax.dynamic_update_index_in_dim(acc, current + product, target, 0)

    terms = lax.fori_loop(
        lower, upper, spread_step, jnp.zeros((tiles_here, tile, width), F32)
    )
    gathered_back = lax.psum_scatter(
        terms.reshape(extent, width).astype(BF16), "col", scatter_dimension=0, tiled=True
    ).astype(F32)
    grad_features = (grad_mid.astype(F32) + gathered_back).astype(BF16)
    share = width // lax.axis_size("col")
    total_weight = lax.psum(local_weight, ("row", "col"))
    grad_weight = lax.dynamic_slice_in_dim(total_weight, lax.axis_index("col") * share, share, 0)
    return (out_features, grad_features, grad_weight)


def swap(value, axis, mask, size):
    return lax.ppermute(value, axis, [(i, i ^ mask) for i in range(size)])


def vmem(count):
    return [pl.BlockSpec(memory_space=pltpu.VMEM)] * count


def place(adj, row, tp, own, slots):
    tile = tp.shape[1]
    for t in range(4):
        name = (own ^ t).astype(F32)
        total = jnp.zeros((tile, tile), F32)
        for s in range(slots):
            mark = tp[pl.ds(slots * tile + 16 * s, 16), :][0:1, :].astype(F32)
            block = tp[pl.ds(s * tile, tile), :]
            total = total + jnp.where(mark == name, block.astype(F32), 0.0)
        adj[pl.ds(row, tile), pl.ds(t * tile, tile)] = total.astype(BF16)


def stage_kernel(slots, where, tp, f, ct, w, f_out, ct_out, w_out, adj):
    place(adj, 0, tp, where[0], slots)
    f_out[...] = f[...]
    ct_out[...] = ct[...]
    w_out[...] = w[...]


def activate(adj, near, far, own_rows, ct, w):
    half = near.shape[0]
    summed = own_rows.astype(F32)
    summed = summed + jnp.dot(adj[:, :half], near, preferred_element_type=F32)
    summed = summed + jnp.dot(adj[:, half:], far, preferred_element_type=F32)
    agg = summed.astype(BF16)
    pre = jnp.dot(agg, w, preferred_element_type=F32)
    sig = jax.nn.sigmoid(pre)
    slope = ct.astype(F32) * sig * (1.0 + pre * (1.0 - sig))
    return agg, pre, slope.astype(BF16)


def own_kernel(f1, f2, f3, f0, adj, ct, w, pre, agg, gp, near, far):
    tile = f1.shape[0]
    near[:tile], near[tile:] = f0[...], f1[...]
    far[:tile], far[tile:] = f2[...], f3[...]
    agg[...], pre[...], gp[...] = activate(adj[...], near[...], far[...], f0[...], ct[...], w[...])


def pair_kernel(scale, slots, where, near, far, tp, ct, w, agg0, gp0,
                gp1, adj, keep, send, agg, gp, gw):
    tile = tp.shape[1]
    own, half = where[0], where[1]
    place(adj, 0, tp, own, slots)
    agg[:tile], gp[:tile] = agg0[...], gp0[...]
    agg1, _, slope = activate(adj[...], near[...], far[...], near[tile:], ct[...], w[...])
    agg[tile:], gp[tile:], gp1[...] = agg1, slope, slope
    part = tile // 2
    for b in range(2):
        lane = pl.multiple_of((own ^ (2 * b)) * tile, tile)
        gw[pl.ds(b * tile, tile), :] = lax.dot_general(
            agg[:, pl.ds(lane, tile)], gp[...], (((0,), (0,)), ((), ())),
            preferred_element_type=F32,
        ) * scale
        mine = pl.multiple_of(b * tile + half * part, part)
        other = pl.multiple_of(b * tile + (1 - half) * part, part)
        keep[b] = gw[pl.ds(mine, part), :]
        send[b] = gw[pl.ds(other, part), :].astype(BF16)


def pack_kernel(index, count, blocks, packed):
    slots, tile, _ = blocks.shape
    for s in range(slots):
        packed[pl.ds(s * tile, tile), :] = blocks[s]
        mark = jnp.where(s < count[0], index[0, s], -1).astype(F32)
        packed[pl.ds(slots * tile + 16 * s, 16), :] = jnp.full((16, tile), mark, F32).astype(BF16)


def backward_kernel(gp0, gp1, adj0, adj1, w, back, part):
    tile = gp0.shape[0]
    terms = jnp.zeros((2 * tile, w.shape[0]), F32)
    for b, (gp, adj) in enumerate(((gp0, adj0), (gp1, adj1))):
        mid = lax.dot_general(
            gp[...], w[...], (((1,), (1,)), ((), ())), preferred_element_type=F32
        ).astype(BF16)
        sel = jnp.concatenate([adj[:, :tile], adj[:, 2 * tile : 3 * tile]], axis=1)
        terms = terms + lax.dot_general(
            sel, mid, (((0,), (0,)), ((), ())), preferred_element_type=F32
        )
        if b == 0:
            part[...] = mid.astype(F32)
    back[...] = terms[tile:].astype(BF16)
    part[...] = part[...] + terms[:tile]


def four_by_eight(features, weight, cotangent, tile_blocks, tile_index, tile_count):
    rows, width = features.shape
    slots, tile, _ = tile_blocks.shape
    own = lax.axis_index("col")
    half = lax.axis_index("row") & 1
    where = jnp.stack([own, half]).astype(jnp.int32)
    f3 = swap(features, "col", 3, 4)
    f2 = swap(features, "col", 2, 4)
    f1 = swap(features, "col", 1, 4)
    ct1 = swap(cotangent, "col", 1, 4)
    tp0 = pl.pallas_call(
        pack_kernel,
        out_shape=jax.ShapeDtypeStruct((slots * (tile + 16), tile), BF16),
        in_specs=[pl.BlockSpec(memory_space=pltpu.SMEM)] * 2 + vmem(1),
        out_specs=vmem(1)[0],
        compiler_params=pltpu.CompilerParams(vmem_limit_bytes=2 << 20),
    )(tile_index, tile_count, tile_blocks)
    tp1 = swap(tp0, "col", 1, 4)
    f0, ct0, w, adj0 = pl.pallas_call(
        functools.partial(stage_kernel, slots),
        out_shape=(
            jax.ShapeDtypeStruct((rows, width), BF16),
            jax.ShapeDtypeStruct((rows, width), BF16),
            jax.ShapeDtypeStruct((width, width), BF16),
            jax.ShapeDtypeStruct((tile, 4 * tile), BF16),
        ),
        in_specs=[pl.BlockSpec(memory_space=pltpu.SMEM)] + vmem(4),
        out_specs=tuple(vmem(4)),
        compiler_params=pltpu.CompilerParams(vmem_limit_bytes=8 << 20),
    )(where, tp0, features, cotangent, weight)
    scale = 1.0 / math.sqrt(rows * lax.axis_size("row") * lax.axis_size("col"))
    block = jax.ShapeDtypeStruct((rows, width), BF16)
    double = jax.ShapeDtypeStruct((2 * rows, width), BF16)
    pre, agg0, gp0, near, far = pl.pallas_call(
        own_kernel,
        out_shape=(jax.ShapeDtypeStruct((rows, width), F32), block, block, double, double),
        in_specs=vmem(7),
        out_specs=tuple(vmem(5)),
        compiler_params=pltpu.CompilerParams(vmem_limit_bytes=8 << 20),
        cost_estimate=pl.CostEstimate(
            flops=4 * rows * width * width, bytes_accessed=1 << 20, transcendentals=rows * width
        ),
    )(f1, f2, f3, f0, adj0, ct0, w)
    gp1, adj1, keep, send = pl.pallas_call(
        functools.partial(pair_kernel, scale, slots),
        out_shape=(
            block,
            jax.ShapeDtypeStruct((tile, 4 * tile), BF16),
            jax.ShapeDtypeStruct((2, tile // 2, width), F32),
            jax.ShapeDtypeStruct((2, tile // 2, width), BF16),
        ),
        in_specs=[pl.BlockSpec(memory_space=pltpu.SMEM)] + vmem(7),
        out_specs=tuple(vmem(4)),
        scratch_shapes=[
            pltpu.VMEM((2 * tile, width), BF16),
            pltpu.VMEM((2 * tile, width), BF16),
            pltpu.VMEM((2 * tile, width), F32),
        ],
        compiler_params=pltpu.CompilerParams(vmem_limit_bytes=12 << 20),
        cost_estimate=pl.CostEstimate(
            flops=8 * rows * width * width, bytes_accessed=2 << 20, transcendentals=rows * width
        ),
    )(where, near, far, tp1, ct1, w, agg0, gp0)
    got = swap(send, "row", 1, 8)
    summed = keep + got.astype(F32)
    pair_term, gp1 = lax.optimization_barrier((summed[1].astype(BF16), gp1))
    got = swap(pair_term, "col", 2, 4)
    mine = (summed[0] + got.astype(F32)).astype(BF16)
    back, part = pl.pallas_call(
        backward_kernel,
        out_shape=(
            jax.ShapeDtypeStruct((rows, width), BF16),
            jax.ShapeDtypeStruct((rows, width), F32),
        ),
        in_specs=vmem(5),
        out_specs=tuple(vmem(2)),
        compiler_params=pltpu.CompilerParams(vmem_limit_bytes=12 << 20),
        cost_estimate=pl.CostEstimate(
            flops=2 * 256 * 512 * 512 * 2, bytes_accessed=2 << 20, transcendentals=0
        ),
    )(gp0, gp1, adj0, adj1, w)
    odd = lax.ppermute(back, "col", [(1, 3), (3, 1)])
    even = lax.ppermute(back, "col", [(0, 2), (2, 0)])
    mine, back = lax.optimization_barrier((mine, back))
    diagonal = swap(mine, "row", 6, 8).astype(F32)
    along = swap(mine, "row", 4, 8).astype(F32)
    across = swap(mine, "row", 2, 8).astype(F32)
    across, even, odd = lax.optimization_barrier((across, even, odd))
    out = (pre * jax.nn.sigmoid(pre)).astype(BF16)
    total = (mine.astype(F32) + across) + (along + diagonal)
    total = total.astype(BF16)
    rest = swap(total, "row", 1, 8)
    grad_features = (part + (odd.astype(F32) + even.astype(F32))).astype(BF16)
    first = jnp.where(half == 0, total, rest)
    second = jnp.where(half == 0, rest, total)
    grad_weight = jnp.concatenate([first, second], axis=0).astype(F32)
    return (out, grad_features, grad_weight)


def solution(mesh):
    sizes = (mesh.shape["row"], mesh.shape["col"])

    def on_device(*args):
        rows, width = args[0].shape
        tile = args[3].shape[1]
        small = sizes == (8, 4) and rows == tile and width == 4 * tile
        return (four_by_eight if small else any_mesh)(*args)

    return jax.shard_map(
        on_device,
        mesh=mesh,
        in_specs=(
            P(("row", "col"), None),
            P(),
            P(("row", "col"), None),
            P(("row", "col"), None, None),
            P(("row", "col"), None),
            P(("row", "col")),
        ),
        out_specs=(P(("row", "col"), None), P(("row", "col"), None), P("col", None)),
        check_vma=False,
    )
```
